128 devices in a mesh: chain: 8 (over x, core), tile: 16 (over z, y).
Axes of the slice: x: 4, y: 4, z: 4, core: 2. Of those that a mesh axis runs over, the one named last changes fastest.
Arguments:
- frames: bfloat16 [16, 64, 128, 384], P('chain', 'tile'), may hold values from -6 to 6
- live_rows: int32 [16], P('tile'), may hold values from 1 to 4, as said below
- gain_first: float32 [384], replicated, may hold values from 0.1 to 1.9
- conv_first: bfloat16 [3, 3, 3, 384, 384], replicated, may hold values from -0.078125 to 0.078125
- gain_second: float32 [384], replicated, may hold values from 0.1 to 1.9
- conv_second: bfloat16 [3, 3, 3, 384, 384], replicated, may hold values from -0.078125 to 0.078125
Outputs:
- decoded: bfloat16 [16, 64, 128, 384], P('chain', 'tile')
The draws below stay inside these ranges and needn't reach their ends.
Inputs may be any that keep to these rules, and one draw needn't show every extreme that they name: `live_rows`: some tile has all 4 rows live.
All inputs are finite; a program needn't handle non-finite values.
Results may differ from the reference program's by a relative error of at most 0.0047.
Values may be sent and summed in bfloat16 or wider, within the bound.
A program may use at most 64 MiB of HBM per device.

```python
import jax
import jax.numpy as jnp
from jax import lax

C = 384
H_DEV = 4
W_COL = 128
TILES = 16
NF = 16
NH = 64


def draw_live_rows(key, part):
    key_values = jax.random.fold_in(key, 11)
    key_place = jax.random.fold_in(key, 23)
    values = jax.random.randint(key_values, (TILES,), 1, H_DEV + 1)
    place = jax.random.randint(key_place, (), 0, TILES)
    return values.at[place].set(H_DEV).astype(jnp.int32)


def block_scale(own_key, extent, pieces, least, largest):
    def one(axis_at, blocks):
        draws = jax.random.uniform(jax.random.fold_in(jax.random.fold_in(own_key, 6), axis_at), (blocks,), jnp.float32, least / len(pieces), largest / len(pieces))
        return jnp.repeat(jnp.exp(draws), extent[axis_at] // blocks).reshape((-1,) + (1,) * (len(extent) - axis_at - 1))

    loudness = one(*pieces[0])
    for cut in pieces[1:]:
        loudness = loudness * one(*cut)
    return loudness


def bell_draw(rng, shape, width, reach, cuts=(), held_as=jnp.bfloat16):
    loudness = block_scale(rng, shape, cuts, -0.22, 0.18) if cuts else 1.0
    entries = jax.random.normal(rng, shape, jnp.float32) * width * loudness
    return jnp.minimum(jnp.maximum(entries, -reach), reach).astype(held_as)


def setup_inputs(seed: int = 0) -> dict:
    splits = jax.random.split(jax.random.key(seed), 7)
    frames = bell_draw(splits[0], (NF, NH, W_COL, C), 1.0, 6.0, ((0, 8), (1, 16)))
    live_rows = draw_live_rows(jax.random.fold_in(splits[6], 71), 0)
    gain_first = jnp.clip(1.0 + 0.18 * jax.random.normal(splits[2], (C,), jnp.float32), 0.1, 1.9)
    conv_first = bell_draw(splits[3], (3, 3, 3, C, C), (27 * C // 2) ** -0.5, 0.078125)
    gain_second = jnp.clip(1.0 + 0.18 * jax.random.normal(splits[4], (C,), jnp.float32), 0.1, 1.9)
    conv_second = bell_draw(splits[5], (3, 3, 3, C, C), (27 * C // 2) ** -0.5, 0.078125)
    return dict(frames=frames, live_rows=live_rows, gain_first=gain_first, conv_first=conv_first, gain_second=gain_second, conv_second=conv_second)


def activate(value, gain):
    value = value.astype(jnp.float32)
    meansq = lax.optimization_barrier(jnp.mean(value * value, axis=-1, keepdims=True))
    return jax.nn.silu(value * jax.lax.rsqrt(meansq + 1e-06) * gain)

def convolve(source, weights):
    padded = jnp.pad(source.astype(jnp.float32), ((2, 0), (1, 1), (1, 1), (0, 0)))
    nframe, nrow, ncol = (source.shape[0], source.shape[1], source.shape[2])
    total = jnp.zeros(source.shape, jnp.float32)
    for kt in range(3):
        for kh in range(3):
            for kw in range(3):
                window = padded[kt:kt + nframe, kh:kh + nrow, kw:kw + ncol]
                total = total + jnp.einsum('fhwc,cd->fhwd', window, weights[kt, kh, kw].astype(jnp.float32))
    return total

def reference(frames, live_rows, gain_first, conv_first, gain_second, conv_second):
    rows = jnp.arange(NH, dtype=jnp.int32)
    limits = jnp.repeat(live_rows, H_DEV)
    mask = (rows % H_DEV < limits).astype(jnp.float32)[None, :, None, None]
    first = (mask * activate(frames, gain_first)).astype(jnp.bfloat16)
    hidden = convolve(first, conv_first)
    second = (mask * activate(hidden, gain_second)).astype(jnp.bfloat16)
    out = convolve(second, conv_second)
    return (mask * (frames.astype(jnp.float32) + out)).astype(jnp.bfloat16)
```

```python
import jax
import jax.numpy as jnp
from jax import lax
from jax.experimental import pallas as pl
from jax.experimental.pallas import tpu as pltpu
from jax.sharding import PartitionSpec as P

MESH = pl.DeviceIdType.MESH


def activate(value, gain, mask):
    meansq = jnp.mean(value * value, axis=-1, keepdims=True)
    half = value * lax.rsqrt(meansq + 1e-06) * (0.5 * gain)
    return (mask * (half + half * jnp.tanh(half))).astype(jnp.bfloat16)


def block_kernel(
    n_chain, n_tile,
    live, frames_hbm, gain1, gain2, conv1_hbm, conv2_hbm, out_hbm,
    frames, a1, a2, w1, w2, part, result,
    in_sem, w_sem, out_sem, send_sem, recv_sem,
):
    c = lax.axis_index("chain")
    t = lax.axis_index("tile")
    nframe, nrow, ncol, width = frames.shape
    taps = 3 * width

    load = pltpu.make_async_copy(frames_hbm, frames, in_sem)
    load.start()
    weight_copies = {}
    for k, (hbm, w) in enumerate(((conv1_hbm, w1), (conv2_hbm, w2))):
        for kt in (2, 1, 0):
            group = []
            for kh in range(3):
                for kw in range(3):
                    group.append(
                        pltpu.make_async_copy(
                            hbm.at[kt, kh, kw],
                            w.at[pl.ds((kt * 3 + kh) * width, width), pl.ds(kw * width, width)],
                            w_sem.at[k, kt, kh, kw],
                        )
                    )
            weight_copies[k, kt] = group
            for copy in group:
                copy.start()

    def need_weights(k, kt):
        for copy in weight_copies[k, kt]:
            copy.wait()

    barrier = pltpu.get_barrier_semaphore()
    for axis, index, count in (("chain", c, n_chain), ("tile", t, n_tile)):
        for step in (1, count - 1):
            pl.semaphore_signal(
                barrier, inc=1, device_id={axis: lax.rem(index + step, count)}, device_id_type=MESH
            )

    even = lax.rem(c, 2) == 0
    after = c > 0
    before = c < n_chain - 1
    above = t > 0
    below = t < n_tile - 1

    for a in (a1, a2):
        @pl.when(c == 0)
        def _():
            a[0:nframe] = jnp.zeros((nframe,) + a.shape[1:], a.dtype)

        @pl.when(t == 0)
        def _():
            for g in range(2 * nframe):
                a[g, 0] = jnp.zeros((ncol, width), a.dtype)

        @pl.when(t == n_tile - 1)
        def _():
            for g in range(2 * nframe):
                a[g, nrow + 1] = jnp.zeros((ncol, width), a.dtype)

    last = nrow + 1

    def route(k, f, kind):
        a = (a1, a2)[k]
        own, old = nframe + f, f
        up, down, onward = {"tile": t - 1}, {"tile": t + 1}, {"chain": c + 1}
        src, src_rows, dst, dst_rows, to, s, r = {
            "x_top": (own, (1, 1), old, (1, 1), onward, 0, 0),
            "x_bottom": (own, (nrow, 1), old, (nrow, 1), onward, 1, 1),
            "x_middle": (own, (2, nrow - 2), old, (2, nrow - 2), onward, 2, 2),
            "y_up": (own, (1, 1), own, (last, 1), up, 3, 3),
            "y_down": (own, (nrow, 1), own, (0, 1), down, 4, 4),
            "c_bottom": (own, (last, 1), old, (last, 1), onward, 5, 5),
            "c_top": (own, (0, 1), old, (0, 1), onward, 6, 6),
            "f_up": (old, (1, 1), old, (last, 1), up, 7, 5),
            "f_down": (old, (nrow, 1), old, (0, 1), down, 8, 6),
        }[kind]
        return pltpu.make_async_remote_copy(
            src_ref=a.at[src, pl.ds(*src_rows)],
            dst_ref=a.at[dst, pl.ds(*dst_rows)],
            send_sem=send_sem.at[k, f, s],
            recv_sem=recv_sem.at[k, f, r],
            device_id=to,
            device_id_type=MESH,
        )

    may_send = {
        "x_top": before, "x_bottom": before, "x_middle": before,
        "y_up": above, "y_down": below,
        "c_bottom": even & below, "c_top": even & above,
        "f_up": even & after & above, "f_down": even & after & below,
    }
    may_hear = {
        "x_top": after, "x_bottom": after, "x_middle": after,
        "y_up": below, "y_down": above,
        "c_bottom": after & below, "c_top": after & above,
    }

    def send(k, f, *kinds):
        for kind in kinds:
            @pl.when(may_send[kind])
            def _():
                route(k, f, kind).start()

    def hear(k, f, *kinds):
        for kind in kinds:
            @pl.when(may_hear[kind])
            def _():
                route(k, f, kind).wait_recv()

    def mask(row):
        return jnp.where(live[0] > row, 1.0, 0.0).astype(jnp.float32)

    def columns(g, rows, a):
        return [jnp.concatenate([a[g, r + kh] for r in rows], axis=0) for kh in range(3)]

    def accumulate(a, w, f, rows, kts, fresh):
        lhs = jnp.concatenate([piece for kt in kts for piece in columns(f + kt, rows, a)], axis=1)
        rhs = w[kts[0] * taps : (kts[-1] + 1) * taps]
        got = jnp.dot(lhs, rhs, preferred_element_type=jnp.float32)
        for at, r in enumerate(rows):
            piece = got[at * ncol : (at + 1) * ncol]
            part[f, r] = piece if fresh else part[f, r] + piece

    col = lax.broadcasted_iota(jnp.int32, (ncol, width), 0)

    def total(f, r):
        left = pltpu.roll(part[f, r, :, 0:width], 1, 0)
        right = pltpu.roll(part[f, r, :, 2 * width : 3 * width], ncol - 1, 0)
        return (
            jnp.where(col == 0, 0.0, left)
            + part[f, r, :, width : 2 * width]
            + jnp.where(col == ncol - 1, 0.0, right)
        )

    load.wait()
    for f in (0, 1):
        for r in (0, 3):
            a1[nframe + f, 1 + r] = activate(frames[f, r].astype(jnp.float32), gain1[...], mask(r))
    pl.semaphore_wait(barrier, 4)
    send(0, 0, "y_up", "y_down")
    send(0, 1, "x_top", "x_bottom", "y_up", "y_down")
    for r in (1, 2):
        a1[nframe + 1, 1 + r] = activate(frames[1, r].astype(jnp.float32), gain1[...], mask(r))
    send(0, 1, "x_middle")
    for r in (1, 2):
        a1[nframe, 1 + r] = activate(frames[0, r].astype(jnp.float32), gain1[...], mask(r))
    send(0, 0, "x_top", "x_bottom", "x_middle")

    inner, outer, every = (1, 2), (0, 3), (0, 1, 2, 3)

    need_weights(0, 2)
    accumulate(a1, w1, 0, inner, (2,), True)
    need_weights(0, 1)
    accumulate(a1, w1, 1, inner, (1, 2), True)
    hear(0, 0, "y_up", "y_down")
    send(0, 0, "c_top", "c_bottom")
    accumulate(a1, w1, 0, outer, (2,), True)
    hear(0, 1, "x_top", "x_bottom")
    send(0, 1, "f_up", "f_down")
    hear(0, 1, "y_up", "y_down")
    send(0, 1, "c_top", "c_bottom")
    accumulate(a1, w1, 1, outer, (1, 2), True)
    hear(0, 1, "x_middle", "c_top", "c_bottom")
    need_weights(0, 0)
    accumulate(a1, w1, 1, every, (0,), False)
    hear(0, 0, "x_top", "x_bottom")
    send(0, 0, "f_up", "f_down")
    for r in outer + inner:
        a2[nframe + 1, 1 + r] = activate(total(1, r), gain2[...], mask(r))
    send(1, 1, "x_top", "x_bottom", "y_up", "y_down", "x_middle")
    hear(0, 0, "x_middle", "c_top", "c_bottom")
    accumulate(a1, w1, 0, every, (0, 1), False)
    for r in outer + inner:
        a2[nframe, 1 + r] = activate(total(0, r), gain2[...], mask(r))
    send(1, 0, "y_up", "y_down", "x_top", "x_bottom", "x_middle")

    hear(1, 1, "y_up", "y_down")
    send(1, 1, "c_top", "c_bottom")
    hear(1, 1, "x_top", "x_bottom")
    send(1, 1, "f_up", "f_down")
    need_weights(1, 2)
    accumulate(a2, w2, 0, inner, (2,), True)
    need_weights(1, 1)
    accumulate(a2, w2, 1, inner, (1, 2), True)
    hear(1, 0, "y_up", "y_down")
    send(1, 0, "c_top", "c_bottom")
    accumulate(a2, w2, 0, outer, (2,), True)
    hear(1, 0, "x_top", "x_bottom")
    send(1, 0, "f_up", "f_down")
    accumulate(a2, w2, 1, outer, (1, 2), True)
    need_weights(1, 0)
    hear(1, 1, "x_middle", "c_top", "c_bottom")
    accumulate(a2, w2, 1, every, (0,), False)

    def finish(f):
        for r in every:
            value = frames[f, r].astype(jnp.float32) + total(f, r)
            result[f, r] = (mask(r) * value).astype(jnp.bfloat16)
        return pltpu.make_async_copy(result.at[f], out_hbm.at[f], out_sem.at[f])

    store1 = finish(1)
    store1.start()
    hear(1, 0, "x_middle", "c_top", "c_bottom")
    accumulate(a2, w2, 0, every, (0, 1), False)
    store0 = finish(0)
    store0.start()

    for k in (0, 1):
        for f in (0, 1):
            for kind in may_send:
                @pl.when(may_send[kind])
                def _():
                    route(k, f, kind).wait_send()
    store1.wait()
    store0.wait()


def shards(frames, live_rows, gain_first, conv_first, gain_second, conv_second):
    nframe, nrow, ncol, width = frames.shape
    halo = (2 * nframe, nrow + 2, ncol, width)
    taps = 9 * width
    vmem, hbm = pltpu.VMEM, pl.ANY
    n_chain, n_tile = lax.axis_size("chain"), lax.axis_size("tile")

    def kernel(*refs):
        block_kernel(n_chain, n_tile, *refs)

    return pl.pallas_call(
        kernel,
        out_shape=jax.ShapeDtypeStruct(frames.shape, frames.dtype),
        in_specs=[
            pl.BlockSpec(memory_space=pltpu.SMEM),
            pl.BlockSpec(memory_space=hbm),
            pl.BlockSpec(memory_space=vmem),
            pl.BlockSpec(memory_space=vmem),
            pl.BlockSpec(memory_space=hbm),
            pl.BlockSpec(memory_space=hbm),
        ],
        out_specs=pl.BlockSpec(memory_space=hbm),
        scratch_shapes=[
            vmem(frames.shape, jnp.bfloat16),
            vmem(halo, jnp.bfloat16),
            vmem(halo, jnp.bfloat16),
            vmem((taps, 3 * width), jnp.bfloat16),
            vmem((taps, 3 * width), jnp.bfloat16),
            vmem((nframe, nrow, ncol, 3 * width), jnp.float32),
            vmem(frames.shape, jnp.bfloat16),
            pltpu.SemaphoreType.DMA,
            pltpu.SemaphoreType.DMA((2, 3, 3, 3)),
            pltpu.SemaphoreType.DMA((2,)),
            pltpu.SemaphoreType.DMA((2, 2, 9)),
            pltpu.SemaphoreType.DMA((2, 2, 7)),
        ],
        compiler_params=pltpu.CompilerParams(
            collective_id=0, has_side_effects=True, vmem_limit_bytes=56 << 20
        ),
    )(
        live_rows,
        frames,
        gain_first.reshape(1, width),
        gain_second.reshape(1, width),
        conv_first,
        conv_second,
    )


def solution(mesh):
    placed = (P("chain", "tile", None, None), P("tile"), P(), P(), P(), P())
    return jax.shard_map(
        shards,
        mesh=mesh,
        in_specs=placed,
        out_specs=P("chain", "tile", None, None),
        check_vma=False,
    )
```

```python
import jax
import jax.numpy as jnp
from jax import lax
from jax.experimental import pallas as pl
from jax.experimental.pallas import tpu as pltpu
from jax.sharding import PartitionSpec as P

MESH = pl.DeviceIdType.MESH


def activate(value, gain, mask):
    meansq = jnp.mean(value * value, axis=-1, keepdims=True)
    half = value * lax.rsqrt(meansq + 1e-06) * (0.5 * gain).reshape(1, -1)
    return (mask * (half + half * jnp.tanh(half))).astype(jnp.bfloat16)


def block_kernel(
    n_chain, n_tile,
    live, frames_hbm, gain1_hbm, gain2_hbm, conv1_hbm, conv2_hbm, result,
    frames, gain1, gain2, a1, a2, w1, w2, part,
    in_sem, w_sem, send_sem, recv_sem,
):
    c = lax.axis_index("chain")
    t = lax.axis_index("tile")
    nframe, nrow, ncol, width = frames.shape
    taps = 3 * width

    loads = [
        pltpu.make_async_copy(src, dst, in_sem.at[i])
        for i, (src, dst) in enumerate(
            ((frames_hbm, frames), (gain1_hbm, gain1), (gain2_hbm, gain2))
        )
    ]
    for load in loads:
        load.start()
    weight_copies = {}
    for k, (hbm, w) in enumerate(((conv1_hbm, w1), (conv2_hbm, w2))):
        for kt in (2, 1, 0):
            group = []
            for kh in range(3):
                for kw in range(3):
                    group.append(
                        pltpu.make_async_copy(
                            hbm.at[kt, kh, kw],
                            w.at[pl.ds(kh * width, width), pl.ds((kt * 3 + kw) * width, width)],
                            w_sem.at[k, kt, kh, kw],
                        )
                    )
            weight_copies[k, kt] = group

    def fetch_weights(k, kt):
        for copy in weight_copies[k, kt]:
            copy.start()

    fetch_weights(0, 2)
    fetch_weights(0, 1)

    def need_weights(k, kt):
        for copy in weight_copies[k, kt]:
            copy.wait()

    barrier = pltpu.get_barrier_semaphore()
    for axis, index, count in (("chain", c, n_chain), ("tile", t, n_tile)):
        for step in (1, count - 1):
            pl.semaphore_signal(
                barrier, inc=1, device_id={axis: lax.rem(index + step, count)}, device_id_type=MESH
            )

    even = lax.rem(c, 2) == 0
    after = c > 0
    before = c < n_chain - 1
    above = t > 0
    below = t < n_tile - 1

    for a in (a1, a2):
        @pl.when(c == 0)
        def _():
            a[0:nframe] = jnp.zeros((nframe,) + a.shape[1:], a.dtype)

        @pl.when(t == 0)
        def _():
            for g in range(2 * nframe):
                a[g, 0] = jnp.zeros((ncol, width), a.dtype)

        @pl.when(t == n_tile - 1)
        def _():
            for g in range(2 * nframe):
                a[g, nrow + 1] = jnp.zeros((ncol, width), a.dtype)

    last = nrow + 1

    def route(k, f, kind):
        a = (a1, a2)[k]
        own, old = nframe + f, f
        up, down, onward = {"tile": t - 1}, {"tile": t + 1}, {"chain": c + 1}
        src, src_rows, dst, dst_rows, to, s, r = {
            "x_top": (own, (1, 1), old, (1, 1), onward, 0, 0),
            "x_bottom": (own, (nrow, 1), old, (nrow, 1), onward, 1, 1),
            "x_middle": (own, (2, nrow - 2), old, (2, nrow - 2), onward, 2, 2),
            "y_up": (own, (1, 1), own, (last, 1), up, 3, 3),
            "y_down": (own, (nrow, 1), own, (0, 1), down, 4, 4),
            "c_bottom": (own, (last, 1), old, (last, 1), onward, 5, 5),
            "c_top": (own, (0, 1), old, (0, 1), onward, 6, 6),
            "f_up": (old, (1, 1), old, (last, 1), up, 7, 5),
            "f_down": (old, (nrow, 1), old, (0, 1), down, 8, 6),
        }[kind]
        return pltpu.make_async_remote_copy(
            src_ref=a.at[src, pl.ds(*src_rows)],
            dst_ref=a.at[dst, pl.ds(*dst_rows)],
            send_sem=send_sem.at[k, f, s],
            recv_sem=recv_sem.at[k, f, r],
            device_id=to,
            device_id_type=MESH,
        )

    may_send = {
        "x_top": before, "x_bottom": before, "x_middle": before,
        "y_up": above, "y_down": below,
        "c_bottom": even & below, "c_top": even & above,
        "f_up": even & after & above, "f_down": even & after & below,
    }
    may_hear = {
        "x_top": after, "x_bottom": after, "x_middle": after,
        "y_up": below, "y_down": above,
        "c_bottom": after & below, "c_top": after & above,
    }

    def send(k, f, *kinds):
        for kind in kinds:
            @pl.when(may_send[kind])
            def _():
                route(k, f, kind).start()

    def hear(k, f, *kinds):
        for kind in kinds:
            @pl.when(may_hear[kind])
            def _():
                route(k, f, kind).wait_recv()

    def mask(row):
        return jnp.where(live[0] > row, 1.0, 0.0).astype(jnp.float32)

    def accumulate(a, w, g, rows):
        lhs = jnp.concatenate(
            [jnp.concatenate([a[g, r + kh] for r in rows], axis=0) for kh in range(3)], axis=1
        )
        kts = [kt for kt in range(3) if 0 <= g - kt < nframe]
        rhs = w[:, kts[0] * taps : (kts[-1] + 1) * taps]
        got = jnp.dot(lhs, rhs, preferred_element_type=jnp.float32)
        for n, kt in enumerate(kts):
            f = g - kt
            fresh = g == nframe + f
            for at, r in enumerate(rows):
                piece = got[at * ncol : (at + 1) * ncol, n * taps : (n + 1) * taps]
                part[f, r] = piece if fresh else part[f, r] + piece

    col = lax.broadcasted_iota(jnp.int32, (ncol, width), 0)

    def total(f, r):
        left = pltpu.roll(part[f, r, :, 0:width], 1, 0)
        right = pltpu.roll(part[f, r, :, 2 * width : 3 * width], ncol - 1, 0)
        return (
            jnp.where(col == 0, 0.0, left)
            + part[f, r, :, width : 2 * width]
            + jnp.where(col == ncol - 1, 0.0, right)
        )

    inner, outer = (1, 2), (0, 3)
    edges, halos, sides = ("x_top", "x_bottom"), ("c_top", "c_bottom"), ("y_up", "y_down")
    forwards = ("f_up", "f_down")

    def first(f, rows):
        for r in rows:
            a1[nframe + f, 1 + r] = activate(frames[f, r].astype(jnp.float32), gain1[...], mask(r))

    def second(f, rows):
        for r in rows:
            a2[nframe + f, 1 + r] = activate(total(f, r), gain2[...], mask(r))

    def decoded(f, rows):
        for r in rows:
            value = frames[f, r].astype(jnp.float32) + total(f, r)
            result[f, r] = (mask(r) * value).astype(jnp.bfloat16)

    for load in loads:
        load.wait()
    first(1, outer)
    pl.semaphore_wait(barrier, 4)
    send(0, 1, *sides, *edges)
    first(1, inner)
    first(0, outer)
    first(0, inner)
    fetch_weights(0, 0)

    need_weights(0, 2)
    accumulate(a1, w1, 3, inner)
    send(0, 1, "x_middle")
    send(0, 0, *sides)
    need_weights(0, 1)
    accumulate(a1, w1, 2, inner)
    send(0, 0, *edges, "x_middle")
    hear(0, 1, *sides)
    send(0, 1, *halos)
    hear(0, 1, *edges)
    send(0, 1, *forwards)
    fetch_weights(1, 2)
    accumulate(a1, w1, 3, outer)
    hear(0, 0, *sides)
    send(0, 0, *halos)
    accumulate(a1, w1, 2, outer)
    hear(0, 1, "x_middle")
    need_weights(0, 0)
    fetch_weights(1, 1)
    accumulate(a1, w1, 1, inner)
    hear(0, 0, *edges)
    send(0, 0, *forwards)
    second(1, inner)
    send(1, 1, "x_middle")
    hear(0, 1, *halos)
    fetch_weights(1, 0)
    accumulate(a1, w1, 1, outer)
    second(1, outer)
    send(1, 1, *sides, *edges)
    hear(0, 0, "x_middle")
    accumulate(a1, w1, 0, inner)
    second(0, inner)
    send(1, 0, "x_middle")
    hear(0, 0, *halos)
    accumulate(a1, w1, 0, outer)
    second(0, outer)
    send(1, 0, *sides, *edges)

    need_weights(1, 2)
    accumulate(a2, w2, 3, inner)
    hear(1, 1, *sides)
    send(1, 1, *halos)
    hear(1, 1, *edges)
    send(1, 1, *forwards)
    need_weights(1, 1)
    accumulate(a2, w2, 2, inner)
    accumulate(a2, w2, 3, outer)
    hear(1, 0, *sides)
    send(1, 0, *halos)
    hear(1, 0, *edges)
    send(1, 0, *forwards)
    accumulate(a2, w2, 2, outer)
    hear(1, 1, "x_middle")
    need_weights(1, 0)
    accumulate(a2, w2, 1, inner)
    hear(1, 1, *halos)
    decoded(1, inner)
    accumulate(a2, w2, 1, outer)
    hear(1, 0, "x_middle")
    decoded(1, outer)
    accumulate(a2, w2, 0, inner)
    hear(1, 0, *halos)
    decoded(0, inner)
    accumulate(a2, w2, 0, outer)
    decoded(0, outer)

    for k in (0, 1):
        for f in (0, 1):
            for kind in may_send:
                @pl.when(may_send[kind])
                def _():
                    route(k, f, kind).wait_send()


def shards(frames, live_rows, gain_first, conv_first, gain_second, conv_second):
    nframe, nrow, ncol, width = frames.shape
    halo = (2 * nframe, nrow + 2, ncol, width)
    taps = 3 * width
    vmem, hbm = pltpu.VMEM, pltpu.HBM
    n_chain, n_tile = lax.axis_size("chain"), lax.axis_size("tile")

    def kernel(*refs):
        block_kernel(n_chain, n_tile, *refs)

    return pl.pallas_call(
        kernel,
        out_shape=jax.ShapeDtypeStruct(frames.shape, frames.dtype),
        in_specs=[
            pl.BlockSpec(memory_space=pltpu.SMEM),
            pl.BlockSpec(memory_space=hbm),
            pl.BlockSpec(memory_space=hbm),
            pl.BlockSpec(memory_space=hbm),
            pl.BlockSpec(memory_space=hbm),
            pl.BlockSpec(memory_space=hbm),
        ],
        out_specs=pl.BlockSpec(memory_space=vmem),
        scratch_shapes=[
            vmem(frames.shape, jnp.bfloat16),
            vmem((width,), jnp.float32),
            vmem((width,), jnp.float32),
            vmem(halo, jnp.bfloat16),
            vmem(halo, jnp.bfloat16),
            vmem((taps, 3 * taps), jnp.bfloat16),
            vmem((taps, 3 * taps), jnp.bfloat16),
            vmem((nframe, nrow, ncol, taps), jnp.float32),
            pltpu.SemaphoreType.DMA((3,)),
            pltpu.SemaphoreType.DMA((2, 3, 3, 3)),
            pltpu.SemaphoreType.DMA((2, 2, 9)),
            pltpu.SemaphoreType.DMA((2, 2, 7)),
        ],
        compiler_params=pltpu.CompilerParams(
            collective_id=0, has_side_effects=True, vmem_limit_bytes=55750000
        ),
    )(
        live_rows,
        frames,
        gain_first,
        gain_second,
        conv_first,
        conv_second,
    )


def solution(mesh):
    placed = (P("chain", "tile", None, None), P("tile"), P(), P(), P(), P())
    return jax.shard_map(
        shards,
        mesh=mesh,
        in_specs=placed,
        out_specs=P("chain", "tile", None, None),
        check_vma=False,
    )
```

```python
import jax
import jax.numpy as jnp
from jax import lax
from jax.experimental import pallas as pl
from jax.experimental.pallas import tpu as pltpu
from jax.sharding import PartitionSpec as P

MESH = pl.DeviceIdType.MESH


def activate(value, gain, mask):
    meansq = jnp.mean(value * value, axis=-1, keepdims=True)
    half = value * lax.rsqrt(meansq + 1e-06) * (0.5 * gain).reshape(1, -1)
    return (mask * (half + half * jnp.tanh(half))).astype(jnp.bfloat16)


def block_kernel(
    n_chain, n_tile,
    live, frames_hbm, gain1_hbm, gain2_hbm, conv1_hbm, conv2_hbm, result,
    frames, gain1, gain2, a1, a2, w1, w2, part,
    in_sem, w_sem, send_sem, recv_sem,
):
    c = lax.axis_index("chain")
    t = lax.axis_index("tile")
    nframe, nrow, ncol, width = frames.shape
    taps = 3 * width

    barrier = pltpu.get_barrier_semaphore()
    for axis, index, count in (("chain", c, n_chain), ("tile", t, n_tile)):
        for step in (1, count - 1):
            pl.semaphore_signal(
                barrier, inc=1, device_id={axis: lax.rem(index + step, count)}, device_id_type=MESH
            )

    loads = [
        pltpu.make_async_copy(src, dst, in_sem.at[i])
        for i, (src, dst) in enumerate(
            ((frames_hbm, frames), (gain1_hbm, gain1), (gain2_hbm, gain2))
        )
    ]
    for load in loads:
        load.start()
    weight_copies = {
        (k, kt): [
            pltpu.make_async_copy(
                hbm.at[kt, :, kw],
                w.at[:, :, pl.ds((kt * 3 + kw) * width, width)],
                w_sem.at[k, kt, kw],
            )
            for kw in range(3)
        ]
        for k, (hbm, w) in enumerate(((conv1_hbm, w1), (conv2_hbm, w2)))
        for kt in range(3)
    }

    def fetch_weights(k, kt):
        for copy in weight_copies[k, kt]:
            copy.start()

    fetch_weights(0, 2)
    fetch_weights(0, 1)

    def need_weights(k, kt):
        for copy in weight_copies[k, kt]:
            copy.wait()

    even = lax.rem(c, 2) == 0
    after = c > 0
    before = c < n_chain - 1
    above = t > 0
    below = t < n_tile - 1

    for a in (a1, a2):
        @pl.when(c == 0)
        def _():
            a[0:nframe] = jnp.zeros((nframe,) + a.shape[1:], a.dtype)

        @pl.when(t == 0)
        def _():
            for g in range(2 * nframe):
                a[g, 0] = jnp.zeros((ncol, width), a.dtype)

        @pl.when(t == n_tile - 1)
        def _():
            for g in range(2 * nframe):
                a[g, nrow + 1] = jnp.zeros((ncol, width), a.dtype)

    last = nrow + 1

    def route(k, f, kind):
        a = (a1, a2)[k]
        own, old = nframe + f, f
        up, down, onward = {"tile": t - 1}, {"tile": t + 1}, {"chain": c + 1}
        src, src_rows, dst, dst_rows, to, s, r = {
            "x_top": (own, (1, 1), old, (1, 1), onward, 0, 0),
            "x_bottom": (own, (nrow, 1), old, (nrow, 1), onward, 1, 1),
            "x_middle": (own, (2, nrow - 2), old, (2, nrow - 2), onward, 2, 2),
            "y_up": (own, (1, 1), own, (last, 1), up, 3, 3),
            "y_down": (own, (nrow, 1), own, (0, 1), down, 4, 4),
            "c_bottom": (own, (last, 1), old, (last, 1), onward, 5, 5),
            "c_top": (own, (0, 1), old, (0, 1), onward, 6, 6),
            "f_up": (old, (1, 1), old, (last, 1), up, 7, 5),
            "f_down": (old, (nrow, 1), old, (0, 1), down, 8, 6),
        }[kind]
        return pltpu.make_async_remote_copy(
            src_ref=a.at[src, pl.ds(*src_rows)],
            dst_ref=a.at[dst, pl.ds(*dst_rows)],
            send_sem=send_sem.at[k, f, s],
            recv_sem=recv_sem.at[k, f, r],
            device_id=to,
            device_id_type=MESH,
        )

    may_send = {
        "x_top": before, "x_bottom": before, "x_middle": before,
        "y_up": above, "y_down": below,
        "c_bottom": even & below, "c_top": even & above,
        "f_up": even & after & above, "f_down": even & after & below,
    }
    may_hear = {
        "x_top": after, "x_bottom": after, "x_middle": after,
        "y_up": below, "y_down": above,
        "c_bottom": after & below, "c_top": after & above,
    }

    def send(k, f, *kinds):
        for kind in kinds:
            @pl.when(may_send[kind])
            def _():
                route(k, f, kind).start()

    def hear(k, f, *kinds):
        for kind in kinds:
            @pl.when(may_hear[kind])
            def _():
                route(k, f, kind).wait_recv()

    def mask(row):
        return jnp.where(live[0] > row, 1.0, 0.0).astype(jnp.float32)

    begun, started = set(), set()

    def accumulate(a, w, g, rows):
        lhs = jnp.concatenate(
            [jnp.concatenate([a[g, r + kh] for r in rows], axis=0) for kh in range(3)], axis=1
        )
        kts = [kt for kt in range(3) if 0 <= g - kt < nframe]
        rhs = w[:, :, kts[0] * taps : (kts[-1] + 1) * taps].reshape(taps, len(kts) * taps)
        got = jnp.dot(lhs, rhs, preferred_element_type=jnp.float32)
        for n, kt in enumerate(kts):
            f = g - kt
            fresh = (a is a2, f, rows) not in begun
            begun.add((a is a2, f, rows))
            for at, r in enumerate(rows):
                piece = got[at * ncol : (at + 1) * ncol, n * taps : (n + 1) * taps]
                part[f, r] = piece if fresh else part[f, r] + piece

    def partly(a, w, g, row, khs):
        lhs = jnp.concatenate([a[g, row + kh] for kh in khs], axis=1)
        kts = [kt for kt in range(3) if 0 <= g - kt < nframe]
        rhs = w[khs[0] : khs[-1] + 1, :, kts[0] * taps : (kts[-1] + 1) * taps].reshape(len(khs) * width, len(kts) * taps)
        got = jnp.dot(lhs, rhs, preferred_element_type=jnp.float32)
        for n, kt in enumerate(kts):
            f = g - kt
            piece = got[:, n * taps : (n + 1) * taps]
            part[f, row] = piece if (f, row) not in started else part[f, row] + piece
            started.add((f, row))

    col = lax.broadcasted_iota(jnp.int32, (ncol, width), 0)

    def total(f, r):
        left = pltpu.roll(part[f, r, :, 0:width], 1, 0)
        right = pltpu.roll(part[f, r, :, 2 * width : 3 * width], ncol - 1, 0)
        return (
            jnp.where(col == 0, 0.0, left)
            + part[f, r, :, width : 2 * width]
            + jnp.where(col == ncol - 1, 0.0, right)
        )

    inner, outer = (1, 2), (0, 3)
    edges, halos, sides = ("x_top", "x_bottom"), ("c_top", "c_bottom"), ("y_up", "y_down")
    forwards = ("f_up", "f_down")

    def first(f, rows):
        for r in rows:
            a1[nframe + f, 1 + r] = activate(frames[f, r].astype(jnp.float32), gain1[...], mask(r))

    def second(f, rows):
        for r in rows:
            a2[nframe + f, 1 + r] = activate(total(f, r), gain2[...], mask(r))

    def decoded(f, rows):
        for r in rows:
            value = frames[f, r].astype(jnp.float32) + total(f, r)
            result[f, r] = (mask(r) * value).astype(jnp.bfloat16)

    for load in loads:
        load.wait()
    first(0, outer)
    first(1, outer)
    pl.semaphore_wait(barrier, 4)
    send(0, 0, *sides)
    send(0, 1, *edges)
    first(1, inner)
    first(0, inner)
    fetch_weights(0, 0)

    need_weights(0, 2)
    accumulate(a1, w1, 3, inner)
    send(0, 1, *sides, "x_middle")
    need_weights(0, 1)
    accumulate(a1, w1, 2, inner)
    send(0, 0, *edges)
    partly(a1, w1, 2, 0, (1, 2))
    partly(a1, w1, 2, 3, (0, 1))
    send(0, 0, "x_middle")
    partly(a1, w1, 3, 0, (1, 2))
    partly(a1, w1, 3, 3, (0, 1))
    hear(0, 0, *sides)
    send(0, 0, *halos)
    hear(0, 1, *edges)
    send(0, 1, *forwards)
    fetch_weights(1, 2)
    partly(a1, w1, 2, 0, (0,))
    partly(a1, w1, 2, 3, (2,))
    hear(0, 1, *sides)
    send(0, 1, *halos)
    partly(a1, w1, 3, 0, (0,))
    partly(a1, w1, 3, 3, (2,))
    begun.update({(False, 0, outer), (False, 1, outer)})
    hear(0, 1, "x_middle")
    need_weights(0, 0)
    fetch_weights(1, 1)
    accumulate(a1, w1, 1, inner)
    hear(0, 0, *edges)
    send(0, 0, *forwards)
    second(1, inner)
    hear(0, 1, *halos)
    fetch_weights(1, 0)
    accumulate(a1, w1, 1, outer)
    second(1, outer)
    send(1, 1, *sides, *edges)
    hear(0, 0, "x_middle")
    need_weights(1, 2)

    @pl.when(even)
    def _():
        accumulate(a1, w1, 0, inner)
        send(1, 1, "x_middle")
        second(0, inner)
        accumulate(a2, w2, 3, inner)
        hear(0, 0, *halos)
        accumulate(a1, w1, 0, outer)
        second(0, outer)
        send(1, 0, *sides, *edges, "x_middle")

    @pl.when(jnp.logical_not(even))
    def _():
        begun.discard((True, 1, inner))
        hear(0, 0, *halos)
        accumulate(a1, w1, 0, outer)
        send(1, 1, "x_middle")
        second(0, outer)
        send(1, 0, *sides, *edges)
        accumulate(a1, w1, 0, inner)
        second(0, inner)
        accumulate(a2, w2, 3, inner)
        send(1, 0, "x_middle")

    hear(1, 1, *sides)
    send(1, 1, *halos)
    hear(1, 1, *edges)
    send(1, 1, *forwards)
    need_weights(1, 1)
    accumulate(a2, w2, 2, inner)
    accumulate(a2, w2, 3, outer)
    hear(1, 1, "x_middle")
    need_weights(1, 0)
    accumulate(a2, w2, 1, inner)
    hear(1, 0, *sides)
    send(1, 0, *halos)
    accumulate(a2, w2, 2, outer)
    hear(1, 0, *edges)
    send(1, 0, *forwards)
    hear(1, 1, *halos)
    decoded(1, inner)
    accumulate(a2, w2, 1, outer)
    hear(1, 0, "x_middle")
    decoded(1, outer)
    accumulate(a2, w2, 0, inner)
    hear(1, 0, *halos)
    decoded(0, inner)
    accumulate(a2, w2, 0, outer)
    decoded(0, outer)

    for k in (0, 1):
        for f in (0, 1):
            for kind in may_send:
                @pl.when(may_send[kind])
                def _():
                    route(k, f, kind).wait_send()


def shards(frames, live_rows, gain_first, conv_first, gain_second, conv_second):
    nframe, nrow, ncol, width = frames.shape
    halo = (2 * nframe, nrow + 2, ncol, width)
    taps = 3 * width
    vmem, hbm = pltpu.VMEM, pltpu.HBM
    n_chain, n_tile = lax.axis_size("chain"), lax.axis_size("tile")

    def kernel(*refs):
        block_kernel(n_chain, n_tile, *refs)

    return pl.pallas_call(
        kernel,
        out_shape=jax.ShapeDtypeStruct(frames.shape, frames.dtype),
        in_specs=[
            pl.BlockSpec(memory_space=pltpu.SMEM),
            pl.BlockSpec(memory_space=hbm),
            pl.BlockSpec(memory_space=hbm),
            pl.BlockSpec(memory_space=hbm),
            pl.BlockSpec(memory_space=hbm),
            pl.BlockSpec(memory_space=hbm),
        ],
        out_specs=pl.BlockSpec(memory_space=vmem),
        scratch_shapes=[
            vmem(frames.shape, jnp.bfloat16),
            vmem((width,), jnp.float32),
            vmem((width,), jnp.float32),
            vmem(halo, jnp.bfloat16),
            vmem(halo, jnp.bfloat16),
            vmem((3, width, 3 * taps), jnp.bfloat16),
            vmem((3, width, 3 * taps), jnp.bfloat16),
            vmem((nframe, nrow, ncol, taps), jnp.float32),
            pltpu.SemaphoreType.DMA((3,)),
            pltpu.SemaphoreType.DMA((2, 3, 3)),
            pltpu.SemaphoreType.DMA((2, 2, 9)),
            pltpu.SemaphoreType.DMA((2, 2, 7)),
        ],
        compiler_params=pltpu.CompilerParams(
            collective_id=0, has_side_effects=True, vmem_limit_bytes=55750000
        ),
    )(
        live_rows,
        frames,
        gain_first,
        gain_second,
        conv_first,
        conv_second,
    )


def solution(mesh):
    placed = (P("chain", "tile", None, None), P("tile"), P(), P(), P(), P())
    return jax.shard_map(
        shards,
        mesh=mesh,
        in_specs=placed,
        out_specs=P("chain", "tile", None, None),
        check_vma=False,
    )
```

```python
import jax
import jax.numpy as jnp
from jax import lax
from jax.experimental import pallas as pl
from jax.experimental.pallas import tpu as pltpu
from jax.sharding import PartitionSpec as P

MESH = pl.DeviceIdType.MESH


def activate(value, gain, mask):
    meansq = jnp.mean(value * value, axis=-1, keepdims=True)
    half = value * lax.rsqrt(meansq + 1e-06) * (0.5 * gain).reshape(1, -1)
    return (mask * (half + half * jnp.tanh(half))).astype(jnp.bfloat16)


def block_kernel(
    n_chain, n_tile,
    live, frames_hbm, gain1_hbm, gain2_hbm, conv1_hbm, conv2_hbm, result,
    frames, gain1, gain2, a1, a2, w1, w2, part,
    in_sem, w_sem, send_sem, recv_sem,
):
    c = lax.axis_index("chain")
    t = lax.axis_index("tile")
    nframe, nrow, ncol, width = frames.shape
    taps = 3 * width

    barrier = pltpu.get_barrier_semaphore()
    for axis, index, count in (("chain", c, n_chain), ("tile", t, n_tile)):
        for step in (1, count - 1):
            pl.semaphore_signal(
                barrier, inc=1, device_id={axis: lax.rem(index + step, count)}, device_id_type=MESH
            )

    loads = [
        pltpu.make_async_copy(src, dst, in_sem.at[i])
        for i, (src, dst) in enumerate(
            ((frames_hbm, frames), (gain1_hbm, gain1), (gain2_hbm, gain2))
        )
    ]
    for load in loads:
        load.start()
    weight_copies = {
        (k, kt): [
            pltpu.make_async_copy(
                hbm.at[kt, :, kw],
                w.at[:, :, pl.ds((kt * 3 + kw) * width, width)],
                w_sem.at[k, kt, kw],
            )
            for kw in range(3)
        ]
        for k, (hbm, w) in enumerate(((conv1_hbm, w1), (conv2_hbm, w2)))
        for kt in range(3)
    }

    def fetch_weights(k, kt):
        for copy in weight_copies[k, kt]:
            copy.start()

    fetch_weights(0, 2)
    fetch_weights(0, 1)

    def need_weights(k, kt):
        for copy in weight_copies[k, kt]:
            copy.wait()

    even = lax.rem(c, 2) == 0
    after = c > 0
    before = c < n_chain - 1
    above = t > 0
    below = t < n_tile - 1

    for a in (a1, a2):
        @pl.when(c == 0)
        def _():
            a[0:nframe] = jnp.zeros((nframe,) + a.shape[1:], a.dtype)

        @pl.when(t == 0)
        def _():
            for g in range(2 * nframe):
                a[g, 0] = jnp.zeros((ncol, width), a.dtype)

        @pl.when(t == n_tile - 1)
        def _():
            for g in range(2 * nframe):
                a[g, nrow + 1] = jnp.zeros((ncol, width), a.dtype)

    last = nrow + 1

    def route(k, f, kind):
        a = (a1, a2)[k]
        own, old = nframe + f, f
        up, down, onward = {"tile": t - 1}, {"tile": t + 1}, {"chain": c + 1}
        src, src_rows, dst, dst_rows, to, s, r = {
            "x_top": (own, (1, 1), old, (1, 1), onward, 0, 0),
            "x_bottom": (own, (nrow, 1), old, (nrow, 1), onward, 1, 1),
            "x_middle": (own, (2, nrow - 2), old, (2, nrow - 2), onward, 2, 2),
            "y_up": (own, (1, 1), own, (last, 1), up, 3, 3),
            "y_down": (own, (nrow, 1), own, (0, 1), down, 4, 4),
            "c_bottom": (own, (last, 1), old, (last, 1), onward, 5, 5),
            "c_top": (own, (0, 1), old, (0, 1), onward, 6, 6),
            "f_up": (old, (1, 1), old, (last, 1), up, 7, 5),
            "f_down": (old, (nrow, 1), old, (0, 1), down, 8, 6),
        }[kind]
        return pltpu.make_async_remote_copy(
            src_ref=a.at[src, pl.ds(*src_rows)],
            dst_ref=a.at[dst, pl.ds(*dst_rows)],
            send_sem=send_sem.at[k, f, s],
            recv_sem=recv_sem.at[k, f, r],
            device_id=to,
            device_id_type=MESH,
        )

    may_send = {
        "x_top": before, "x_bottom": before, "x_middle": before,
        "y_up": above, "y_down": below,
        "c_bottom": even & below, "c_top": even & above,
        "f_up": even & after & above, "f_down": even & after & below,
    }
    may_hear = {
        "x_top": after, "x_bottom": after, "x_middle": after,
        "y_up": below, "y_down": above,
        "c_bottom": after & below, "c_top": after & above,
    }

    def send(k, f, *kinds):
        for kind in kinds:
            @pl.when(may_send[kind])
            def _():
                route(k, f, kind).start()

    def hear(k, f, *kinds):
        for kind in kinds:
            @pl.when(may_hear[kind])
            def _():
                route(k, f, kind).wait_recv()

    def mask(row):
        return jnp.where(live[0] > row, 1.0, 0.0).astype(jnp.float32)

    begun, started = set(), set()

    def accumulate(a, w, g, rows):
        lhs = jnp.concatenate(
            [jnp.concatenate([a[g, r + kh] for r in rows], axis=0) for kh in range(3)], axis=1
        )
        kts = [kt for kt in range(3) if 0 <= g - kt < nframe]
        rhs = w[:, :, kts[0] * taps : (kts[-1] + 1) * taps].reshape(taps, len(kts) * taps)
        got = jnp.dot(lhs, rhs, preferred_element_type=jnp.float32)
        for n, kt in enumerate(kts):
            f = g - kt
            fresh = (a is a2, f, rows) not in begun
            begun.add((a is a2, f, rows))
            for at, r in enumerate(rows):
                piece = got[at * ncol : (at + 1) * ncol, n * taps : (n + 1) * taps]
                part[f, r] = piece if fresh else part[f, r] + piece

    def partly(a, w, g, row, khs):
        lhs = jnp.concatenate([a[g, row + kh] for kh in khs], axis=1)
        kts = [kt for kt in range(3) if 0 <= g - kt < nframe]
        rhs = w[khs[0] : khs[-1] + 1, :, kts[0] * taps : (kts[-1] + 1) * taps].reshape(len(khs) * width, len(kts) * taps)
        got = jnp.dot(lhs, rhs, preferred_element_type=jnp.float32)
        for n, kt in enumerate(kts):
            f = g - kt
            piece = got[:, n * taps : (n + 1) * taps]
            part[f, row] = piece if (f, row) not in started else part[f, row] + piece
            started.add((f, row))

    col = lax.broadcasted_iota(jnp.int32, (ncol, width), 0)

    def total(f, r):
        left = pltpu.roll(part[f, r, :, 0:width], 1, 0)
        right = pltpu.roll(part[f, r, :, 2 * width : 3 * width], ncol - 1, 0)
        return (
            jnp.where(col == 0, 0.0, left)
            + part[f, r, :, width : 2 * width]
            + jnp.where(col == ncol - 1, 0.0, right)
        )

    inner, outer = (1, 2), (0, 3)
    edges, halos, sides = ("x_top", "x_bottom"), ("c_top", "c_bottom"), ("y_up", "y_down")
    forwards = ("f_up", "f_down")

    def first(f, rows):
        for r in rows:
            a1[nframe + f, 1 + r] = activate(frames[f, r].astype(jnp.float32), gain1[...], mask(r))

    def second(f, rows):
        for r in rows:
            a2[nframe + f, 1 + r] = activate(total(f, r), gain2[...], mask(r))

    def decoded(f, rows):
        for r in rows:
            value = frames[f, r].astype(jnp.float32) + total(f, r)
            result[f, r] = (mask(r) * value).astype(jnp.bfloat16)

    for load in loads:
        load.wait()
    first(0, outer)
    first(1, outer)
    pl.semaphore_wait(barrier, 4)
    send(0, 0, *sides)
    send(0, 1, *edges)
    first(1, inner)
    first(0, inner)
    fetch_weights(0, 0)

    need_weights(0, 2)
    accumulate(a1, w1, 3, inner)
    send(0, 1, *sides, "x_middle")
    need_weights(0, 1)
    accumulate(a1, w1, 2, inner)
    send(0, 0, *edges)
    partly(a1, w1, 2, 0, (1, 2))
    partly(a1, w1, 2, 3, (0, 1))
    send(0, 0, "x_middle")
    partly(a1, w1, 3, 0, (1, 2))
    partly(a1, w1, 3, 3, (0, 1))
    hear(0, 0, *sides)
    send(0, 0, *halos)
    hear(0, 1, *edges)
    send(0, 1, *forwards)
    fetch_weights(1, 2)
    partly(a1, w1, 2, 0, (0,))
    partly(a1, w1, 2, 3, (2,))
    hear(0, 1, *sides)
    send(0, 1, *halos)
    partly(a1, w1, 3, 0, (0,))
    partly(a1, w1, 3, 3, (2,))
    begun.update({(False, 0, outer), (False, 1, outer)})
    hear(0, 1, "x_middle")
    need_weights(0, 0)
    fetch_weights(1, 1)
    accumulate(a1, w1, 1, inner)
    hear(0, 0, *edges)
    send(0, 0, *forwards)
    second(1, inner)
    hear(0, 1, *halos)
    fetch_weights(1, 0)
    accumulate(a1, w1, 1, outer)
    second(1, outer)
    send(1, 1, *sides, *edges)
    hear(0, 0, "x_middle")
    need_weights(1, 2)

    @pl.when(even)
    def _():
        accumulate(a1, w1, 0, inner)
        send(1, 1, "x_middle")
        second(0, inner)
        accumulate(a2, w2, 3, inner)
        hear(0, 0, *halos)
        accumulate(a1, w1, 0, outer)
        second(0, outer)
        send(1, 0, *sides, *edges, "x_middle")

    @pl.when(jnp.logical_not(even))
    def _():
        begun.discard((True, 1, inner))
        hear(0, 0, *halos)
        accumulate(a1, w1, 0, outer)
        send(1, 1, "x_middle")
        second(0, outer)
        send(1, 0, *sides, *edges)
        accumulate(a1, w1, 0, inner)
        second(0, inner)
        accumulate(a2, w2, 3, inner)
        send(1, 0, "x_middle")

    hear(1, 1, *sides)
    send(1, 1, *halos)
    hear(1, 1, *edges)
    send(1, 1, *forwards)
    need_weights(1, 1)
    accumulate(a2, w2, 2, inner)
    accumulate(a2, w2, 3, outer)
    hear(1, 1, "x_middle")
    need_weights(1, 0)
    accumulate(a2, w2, 1, inner)
    begun.update({(True, 0, outer), (True, 1, outer)})
    started.difference_update({(0, 0), (0, 3)})
    partly(a2, w2, 2, 0, (1, 2))
    partly(a2, w2, 2, 3, (0, 1))
    hear(1, 0, *sides)
    send(1, 0, *halos)
    hear(1, 0, *edges)
    send(1, 0, *forwards)
    partly(a2, w2, 2, 0, (0,))
    partly(a2, w2, 2, 3, (2,))
    hear(1, 1, *halos)
    decoded(1, inner)
    accumulate(a2, w2, 1, outer)
    hear(1, 0, "x_middle")
    decoded(1, outer)
    accumulate(a2, w2, 0, inner)
    partly(a2, w2, 0, 0, (1, 2))
    partly(a2, w2, 0, 3, (0, 1))
    decoded(0, inner)
    hear(1, 0, *halos)
    partly(a2, w2, 0, 0, (0,))
    partly(a2, w2, 0, 3, (2,))
    decoded(0, outer)

    for k in (0, 1):
        for f in (0, 1):
            for kind in may_send:
                @pl.when(may_send[kind])
                def _():
                    route(k, f, kind).wait_send()


def shards(frames, live_rows, gain_first, conv_first, gain_second, conv_second):
    nframe, nrow, ncol, width = frames.shape
    halo = (2 * nframe, nrow + 2, ncol, width)
    taps = 3 * width
    vmem, hbm = pltpu.VMEM, pltpu.HBM
    n_chain, n_tile = lax.axis_size("chain"), lax.axis_size("tile")

    def kernel(*refs):
        block_kernel(n_chain, n_tile, *refs)

    return pl.pallas_call(
        kernel,
        out_shape=jax.ShapeDtypeStruct(frames.shape, frames.dtype),
        in_specs=[
            pl.BlockSpec(memory_space=pltpu.SMEM),
            pl.BlockSpec(memory_space=hbm),
            pl.BlockSpec(memory_space=hbm),
            pl.BlockSpec(memory_space=hbm),
            pl.BlockSpec(memory_space=hbm),
            pl.BlockSpec(memory_space=hbm),
        ],
        out_specs=pl.BlockSpec(memory_space=vmem),
        scratch_shapes=[
            vmem(frames.shape, jnp.bfloat16),
            vmem((width,), jnp.float32),
            vmem((width,), jnp.float32),
            vmem(halo, jnp.bfloat16),
            vmem(halo, jnp.bfloat16),
            vmem((3, width, 3 * taps), jnp.bfloat16),
            vmem((3, width, 3 * taps), jnp.bfloat16),
            vmem((nframe, nrow, ncol, taps), jnp.float32),
            pltpu.SemaphoreType.DMA((3,)),
            pltpu.SemaphoreType.DMA((2, 3, 3)),
            pltpu.SemaphoreType.DMA((2, 2, 9)),
            pltpu.SemaphoreType.DMA((2, 2, 7)),
        ],
        compiler_params=pltpu.CompilerParams(
            collective_id=0, has_side_effects=True, vmem_limit_bytes=55750000
        ),
    )(
        live_rows,
        frames,
        gain_first,
        gain_second,
        conv_first,
        conv_second,
    )


def solution(mesh):
    placed = (P("chain", "tile", None, None), P("tile"), P(), P(), P(), P())
    return jax.shard_map(
        shards,
        mesh=mesh,
        in_specs=placed,
        out_specs=P("chain", "tile", None, None),
        check_vma=False,
    )
```

```python
import jax
import jax.numpy as jnp
from jax import lax
from jax.experimental import pallas as pl
from jax.experimental.pallas import tpu as pltpu
from jax.sharding import PartitionSpec as P

MESH = pl.DeviceIdType.MESH


def activate(value, gain, mask):
    meansq = jnp.mean(value * value, axis=-1, keepdims=True)
    half = value * lax.rsqrt(meansq + 1e-06) * (0.5 * gain).reshape(1, -1)
    return (mask * (half + half * jnp.tanh(half))).astype(jnp.bfloat16)


def block_kernel(
    n_chain, n_tile,
    live, frames_hbm, gain1_hbm, gain2_hbm, conv1_hbm, conv2_hbm, result,
    frames, gain1, gain2, a1, a2, w1, w2, part,
    in_sem, w_sem, send_sem, recv_sem,
):
    c = lax.axis_index("chain")
    t = lax.axis_index("tile")
    nframe, nrow, ncol, width = frames.shape
    taps = 3 * width

    barrier = pltpu.get_barrier_semaphore()
    for axis, index, count in (("chain", c, n_chain), ("tile", t, n_tile)):
        for step in (1, count - 1):
            pl.semaphore_signal(
                barrier, inc=1, device_id={axis: lax.rem(index + step, count)}, device_id_type=MESH
            )

    loads = [
        pltpu.make_async_copy(src, dst, in_sem.at[i])
        for i, (src, dst) in enumerate(
            ((frames_hbm, frames), (gain1_hbm, gain1), (gain2_hbm, gain2))
        )
    ]
    for load in loads:
        load.start()
    weight_copies = {
        (k, kt): [
            pltpu.make_async_copy(
                hbm.at[kt, :, kw],
                w.at[:, :, pl.ds((kt * 3 + kw) * width, width)],
                w_sem.at[k, kt, kw],
            )
            for kw in range(3)
        ]
        for k, (hbm, w) in enumerate(((conv1_hbm, w1), (conv2_hbm, w2)))
        for kt in range(3)
    }

    def fetch_weights(k, kt):
        for copy in weight_copies[k, kt]:
            copy.start()

    fetch_weights(0, 2)
    fetch_weights(0, 1)

    def need_weights(k, kt):
        for copy in weight_copies[k, kt]:
            copy.wait()

    even = lax.rem(c, 2) == 0
    after = c > 0
    before = c < n_chain - 1
    above = t > 0
    below = t < n_tile - 1

    for a in (a1, a2):
        @pl.when(c == 0)
        def _():
            a[0:nframe] = jnp.zeros((nframe,) + a.shape[1:], a.dtype)

        @pl.when(t == 0)
        def _():
            for g in range(2 * nframe):
                a[g, 0] = jnp.zeros((ncol, width), a.dtype)

        @pl.when(t == n_tile - 1)
        def _():
            for g in range(2 * nframe):
                a[g, nrow + 1] = jnp.zeros((ncol, width), a.dtype)

    last = nrow + 1

    def route(k, f, kind):
        a = (a1, a2)[k]
        own, old = nframe + f, f
        up, down, onward = {"tile": t - 1}, {"tile": t + 1}, {"chain": c + 1}
        src, src_rows, dst, dst_rows, to, s, r = {
            "x_top": (own, (1, 1), old, (1, 1), onward, 0, 0),
            "x_bottom": (own, (nrow, 1), old, (nrow, 1), onward, 1, 1),
            "x_middle": (own, (2, nrow - 2), old, (2, nrow - 2), onward, 2, 2),
            "y_up": (own, (1, 1), own, (last, 1), up, 3, 3),
            "y_down": (own, (nrow, 1), own, (0, 1), down, 4, 4),
            "c_bottom": (own, (last, 1), old, (last, 1), onward, 5, 5),
            "c_top": (own, (0, 1), old, (0, 1), onward, 6, 6),
            "f_up": (old, (1, 1), old, (last, 1), up, 7, 5),
            "f_down": (old, (nrow, 1), old, (0, 1), down, 8, 6),
        }[kind]
        return pltpu.make_async_remote_copy(
            src_ref=a.at[src, pl.ds(*src_rows)],
            dst_ref=a.at[dst, pl.ds(*dst_rows)],
            send_sem=send_sem.at[k, f, s],
            recv_sem=recv_sem.at[k, f, r],
            device_id=to,
            device_id_type=MESH,
        )

    may_send = {
        "x_top": before, "x_bottom": before, "x_middle": before,
        "y_up": above, "y_down": below,
        "c_bottom": even & below, "c_top": even & above,
        "f_up": even & after & above, "f_down": even & after & below,
    }
    may_hear = {
        "x_top": after, "x_bottom": after, "x_middle": after,
        "y_up": below, "y_down": above,
        "c_bottom": after & below, "c_top": after & above,
    }

    def send(k, f, *kinds):
        for kind in kinds:
            @pl.when(may_send[kind])
            def _():
                route(k, f, kind).start()

    def hear(k, f, *kinds):
        for kind in kinds:
            @pl.when(may_hear[kind])
            def _():
                route(k, f, kind).wait_recv()

    def mask(row):
        return jnp.where(live[0] > row, 1.0, 0.0).astype(jnp.float32)

    begun, started = set(), set()

    def accumulate(a, w, g, rows):
        lhs = jnp.concatenate(
            [jnp.concatenate([a[g, r + kh] for r in rows], axis=0) for kh in range(3)], axis=1
        )
        kts = [kt for kt in range(3) if 0 <= g - kt < nframe]
        rhs = w[:, :, kts[0] * taps : (kts[-1] + 1) * taps].reshape(taps, len(kts) * taps)
        got = jnp.dot(lhs, rhs, preferred_element_type=jnp.float32)
        for n, kt in enumerate(kts):
            f = g - kt
            fresh = (a is a2, f, rows) not in begun
            begun.add((a is a2, f, rows))
            for at, r in enumerate(rows):
                piece = got[at * ncol : (at + 1) * ncol, n * taps : (n + 1) * taps]
                part[f, r] = piece if fresh else part[f, r] + piece

    def partly(a, w, g, row, khs):
        lhs = jnp.concatenate([a[g, row + kh] for kh in khs], axis=1)
        kts = [kt for kt in range(3) if 0 <= g - kt < nframe]
        rhs = w[khs[0] : khs[-1] + 1, :, kts[0] * taps : (kts[-1] + 1) * taps].reshape(len(khs) * width, len(kts) * taps)
        got = jnp.dot(lhs, rhs, preferred_element_type=jnp.float32)
        for n, kt in enumerate(kts):
            f = g - kt
            piece = got[:, n * taps : (n + 1) * taps]
            part[f, row] = piece if (f, row) not in started else part[f, row] + piece
            started.add((f, row))

    col = lax.broadcasted_iota(jnp.int32, (ncol, width), 0)

    def total(f, r):
        left = pltpu.roll(part[f, r, :, 0:width], 1, 0)
        right = pltpu.roll(part[f, r, :, 2 * width : 3 * width], ncol - 1, 0)
        return (
            jnp.where(col == 0, 0.0, left)
            + part[f, r, :, width : 2 * width]
            + jnp.where(col == ncol - 1, 0.0, right)
        )

    inner, outer = (1, 2), (0, 3)
    edges, halos, sides = ("x_top", "x_bottom"), ("c_top", "c_bottom"), ("y_up", "y_down")
    forwards = ("f_up", "f_down")

    def first(f, rows):
        for r in rows:
            a1[nframe + f, 1 + r] = activate(frames[f, r].astype(jnp.float32), gain1[...], mask(r))

    def second(f, rows):
        for r in rows:
            a2[nframe + f, 1 + r] = activate(total(f, r), gain2[...], mask(r))

    def decoded(f, rows):
        for r in rows:
            value = frames[f, r].astype(jnp.float32) + total(f, r)
            result[f, r] = (mask(r) * value).astype(jnp.bfloat16)

    for load in loads:
        load.wait()
    first(0, outer)
    first(1, outer)
    pl.semaphore_wait(barrier, 4)
    send(0, 0, *sides)
    send(0, 1, *edges)
    first(1, inner)
    first(0, inner)
    fetch_weights(0, 0)

    need_weights(0, 2)
    accumulate(a1, w1, 3, inner)
    send(0, 1, *sides, "x_middle")
    need_weights(0, 1)
    accumulate(a1, w1, 2, inner)
    send(0, 0, *edges)
    partly(a1, w1, 2, 0, (1, 2))
    partly(a1, w1, 2, 3, (0, 1))
    send(0, 0, "x_middle")
    partly(a1, w1, 3, 0, (1, 2))
    partly(a1, w1, 3, 3, (0, 1))
    hear(0, 0, *sides)
    send(0, 0, *halos)
    hear(0, 1, *edges)
    send(0, 1, *forwards)
    fetch_weights(1, 2)
    partly(a1, w1, 2, 0, (0,))
    partly(a1, w1, 2, 3, (2,))
    hear(0, 1, *sides)
    send(0, 1, *halos)
    partly(a1, w1, 3, 0, (0,))
    partly(a1, w1, 3, 3, (2,))
    begun.update({(False, 0, outer), (False, 1, outer)})
    hear(0, 1, "x_middle")
    need_weights(0, 0)
    fetch_weights(1, 1)
    accumulate(a1, w1, 1, inner)
    hear(0, 0, *edges)
    send(0, 0, *forwards)
    second(1, inner)
    hear(0, 1, *halos)
    fetch_weights(1, 0)
    accumulate(a1, w1, 1, outer)
    second(1, outer)
    send(1, 1, *sides, *edges)
    hear(0, 0, "x_middle")
    need_weights(1, 2)

    @pl.when(even)
    def _():
        accumulate(a1, w1, 0, inner)
        send(1, 1, "x_middle")
        second(0, inner)
        accumulate(a2, w2, 3, inner)
        hear(0, 0, *halos)
        accumulate(a1, w1, 0, outer)
        second(0, outer)
        send(1, 0, *sides, *edges, "x_middle")

    @pl.when(jnp.logical_not(even))
    def _():
        begun.discard((True, 1, inner))
        hear(0, 0, *halos)
        accumulate(a1, w1, 0, outer)
        send(1, 1, "x_middle")
        second(0, outer)
        send(1, 0, *sides, *edges)
        accumulate(a1, w1, 0, inner)
        second(0, inner)
        accumulate(a2, w2, 3, inner)
        send(1, 0, "x_middle")

    hear(1, 1, *sides)
    send(1, 1, *halos)
    hear(1, 1, *edges)
    send(1, 1, *forwards)
    need_weights(1, 1)
    accumulate(a2, w2, 2, inner)
    accumulate(a2, w2, 3, outer)
    hear(1, 1, "x_middle")
    need_weights(1, 0)
    accumulate(a2, w2, 1, inner)
    begun.update({(True, 0, outer), (True, 1, outer)})
    started.difference_update({(0, 0), (0, 3)})
    partly(a2, w2, 2, 0, (1, 2))
    partly(a2, w2, 2, 3, (0, 1))
    hear(1, 0, *sides)
    send(1, 0, *halos)
    hear(1, 0, *edges)
    send(1, 0, *forwards)
    partly(a2, w2, 2, 0, (0,))
    partly(a2, w2, 2, 3, (2,))
    hear(1, 1, *halos)
    decoded(1, inner)
    accumulate(a2, w2, 1, outer)
    hear(1, 0, "x_middle")
    decoded(1, outer)
    accumulate(a2, w2, 0, inner)
    partly(a2, w2, 0, 0, (1, 2))
    partly(a2, w2, 0, 3, (0, 1))
    decoded(0, inner)
    for k in (0, 1):
        for f in (0, 1):
            for kind in may_send:
                @pl.when(may_send[kind])
                def _():
                    route(k, f, kind).wait_send()
    hear(1, 0, *halos)
    partly(a2, w2, 0, 0, (0,))
    partly(a2, w2, 0, 3, (2,))
    decoded(0, outer)


def shards(frames, live_rows, gain_first, conv_first, gain_second, conv_second):
    nframe, nrow, ncol, width = frames.shape
    halo = (2 * nframe, nrow + 2, ncol, width)
    taps = 3 * width
    vmem, hbm = pltpu.VMEM, pltpu.HBM
    n_chain, n_tile = lax.axis_size("chain"), lax.axis_size("tile")

    def kernel(*refs):
        block_kernel(n_chain, n_tile, *refs)

    return pl.pallas_call(
        kernel,
        out_shape=jax.ShapeDtypeStruct(frames.shape, frames.dtype),
        in_specs=[
            pl.BlockSpec(memory_space=pltpu.SMEM),
            pl.BlockSpec(memory_space=hbm),
            pl.BlockSpec(memory_space=hbm),
            pl.BlockSpec(memory_space=hbm),
            pl.BlockSpec(memory_space=hbm),
            pl.BlockSpec(memory_space=hbm),
        ],
        out_specs=pl.BlockSpec(memory_space=vmem),
        scratch_shapes=[
            vmem(frames.shape, jnp.bfloat16),
            vmem((width,), jnp.float32),
            vmem((width,), jnp.float32),
            vmem(halo, jnp.bfloat16),
            vmem(halo, jnp.bfloat16),
            vmem((3, width, 3 * taps), jnp.bfloat16),
            vmem((3, width, 3 * taps), jnp.bfloat16),
            vmem((nframe, nrow, ncol, taps), jnp.float32),
            pltpu.SemaphoreType.DMA((3,)),
            pltpu.SemaphoreType.DMA((2, 3, 3)),
            pltpu.SemaphoreType.DMA((2, 2, 9)),
            pltpu.SemaphoreType.DMA((2, 2, 7)),
        ],
        compiler_params=pltpu.CompilerParams(
            collective_id=0, has_side_effects=True, vmem_limit_bytes=55750000
        ),
    )(
        live_rows,
        frames,
        gain_first,
        gain_second,
        conv_first,
        conv_second,
    )


def solution(mesh):
    placed = (P("chain", "tile", None, None), P("tile"), P(), P(), P(), P())
    return jax.shard_map(
        shards,
        mesh=mesh,
        in_specs=placed,
        out_specs=P("chain", "tile", None, None),
        check_vma=False,
    )
```
